32 devices in a mesh: rep: 8 (over z, x), shard: 4 (over y, core).
Axes of the slice: x: 2, y: 2, z: 4, core: 2. Of those that a mesh axis runs over, the one named last changes fastest.
Arguments:
- tokens: bfloat16 [16384, 1024], P(('rep', 'shard')), may hold values from -6 to 6
- cotangent: bfloat16 [16384, 1024], P(('rep', 'shard')), may hold values from -6 to 6
- block_of: int32 [16, 8], P('rep'), may hold values from 0 to 7, each once within a row
- ln1_gain: bfloat16 [1024], P('shard'), may hold values from 0.5 to 1.5
- ln1_bias: bfloat16 [1024], P('shard'), may hold values from -3 to 3
- ln2_gain: bfloat16 [1024], P('shard'), may hold values from 0.5 to 1.5
- ln2_bias: bfloat16 [1024], P('shard'), may hold values from -3 to 3
- w_qkv: bfloat16 [1024, 3072], P('shard'), may hold values from -0.1875 to 0.1875
- q_bias: bfloat16 [1024], P('shard'), may hold values from -3 to 3
- v_bias: bfloat16 [1024], P('shard'), may hold values from -3 to 3
- w_out: bfloat16 [1024, 1024], P('shard'), may hold values from -0.75 to 0.75
- out_bias: bfloat16 [1024], P('shard'), may hold values from -3 to 3
- w_up: bfloat16 [1024, 4096], P('shard'), may hold values from -0.1875 to 0.1875
- up_bias: bfloat16 [4096], P('shard'), may hold values from -3 to 3
- w_down: bfloat16 [4096, 1024], P('shard'), may hold values from -0.09375 to 0.09375
- down_bias: bfloat16 [1024], P('shard'), may hold values from -3 to 3
Outputs:
- output: bfloat16 [16384, 1024], P(('rep', 'shard'))
- input_grad: float32 [16384, 1024], P(('rep', 'shard'))
- grad_ln1_gain: float32 [1024], P('shard')
- grad_ln1_bias: float32 [1024], P('shard')
- grad_ln2_gain: float32 [1024], P('shard')
- grad_ln2_bias: float32 [1024], P('shard')
- grad_w_qkv: float32 [1024, 3072], P('shard')
- grad_q_bias: float32 [1024], P('shard')
- grad_v_bias: float32 [1024], P('shard')
- grad_w_out: float32 [1024, 1024], P('shard')
- grad_out_bias: float32 [1024], P('shard')
- grad_w_up: float32 [1024, 4096], P('shard')
- grad_up_bias: float32 [4096], P('shard')
- grad_w_down: float32 [4096, 1024], P('shard')
- grad_down_bias: float32 [1024], P('shard')
The draws below stay inside these ranges and needn't reach their ends.
Inputs may be any that keep to these rules, and one draw needn't show every extreme that they name: Each row of block_of names every block of its sequence once; slot j of a sequence lies on index j // 2 of shard.
All inputs are finite; a program needn't handle non-finite values.
Results may differ from the reference program's by a relative error of at most 0.012.
Values may be sent and summed in bfloat16 or wider, within the bound.
No kernel may reach another device: no remote copies, remote signals or barrier semaphores. Data moves between devices by JAX's collectives and lax.ppermute only.
A program may use at most 192 MiB of HBM per device.

```python
import math
import jax
import jax.numpy as jnp
from jax import lax

D = 1024
HEADS = 16
HEAD = 64
FF = 4096
ROT = 16
SEQS = 2
BLOCKS = 8
BLOCK_LEN = 128
SEQ_ALL = 16
TOKENS = 16384
N_REP = 8
N_SHARD = 4


def level_of(key, shape, cuts, least, top_value):
    loudness = 1.0
    for position, blocks in cuts:
        draws = jax.random.uniform(jax.random.fold_in(jax.random.fold_in(key, 6), position), (blocks,), jnp.float32, least / len(cuts), top_value / len(cuts))
        loudness = loudness * jnp.repeat(jnp.exp(draws), shape[position] // blocks).reshape((-1,) + (1,) * (len(shape) - 1 - position))
    return loudness


def bell_draw(rng, extent, width, limit, pieces=(), held_as=jnp.bfloat16):
    values = jax.random.normal(rng, extent, jnp.float32) * width
    if len(pieces) > 0:
        values = level_of(rng, extent, pieces, -0.22, 0.18) * values
    return jnp.clip(values, min=-limit, max=limit).astype(held_as)


def setup_inputs(seed: int = 0) -> dict:
    splits = jax.random.split(jax.random.key(seed), 17)
    return {
        "tokens": bell_draw(splits[0], (TOKENS, D), 1.0, 6.0, ((0, 32),)),
        "cotangent": bell_draw(splits[1], (TOKENS, D), 1.0, 6.0, ((0, 32),)),
        "block_of": jax.vmap(lambda own: jax.random.permutation(own, BLOCKS))(jax.random.split(splits[2], SEQ_ALL)).reshape((SEQ_ALL, BLOCKS)).astype(jnp.int32),
        "ln1_gain": jnp.clip(1.0 + 0.1 * jax.random.normal(splits[3], (D,), jnp.float32), 0.5, 1.5).astype(jnp.bfloat16),
        "ln1_bias": bell_draw(splits[4], (D,), 0.5, 3.0, ((0, 4),)),
        "ln2_gain": jnp.clip(1.0 + 0.1 * jax.random.normal(splits[5], (D,), jnp.float32), 0.5, 1.5).astype(jnp.bfloat16),
        "ln2_bias": bell_draw(splits[6], (D,), 0.5, 3.0, ((0, 4),)),
        "w_qkv": bell_draw(splits[7], (D, 3 * D), D ** -0.5, 0.1875, ((0, 4),)),
        "q_bias": bell_draw(splits[8], (D,), 0.5, 3.0, ((0, 4),)),
        "v_bias": bell_draw(splits[9], (D,), 0.5, 3.0, ((0, 4),)),
        "w_out": bell_draw(splits[10], (D, D), (D // 16) ** -0.5, 0.75, ((0, 4),)),
        "out_bias": bell_draw(splits[11], (D,), 0.5, 3.0, ((0, 4),)),
        "w_up": bell_draw(splits[12], (D, FF), D ** -0.5, 0.1875, ((0, 4),)),
        "up_bias": bell_draw(splits[13], (FF,), 0.5, 3.0, ((0, 4),)),
        "w_down": bell_draw(splits[14], (FF, D), FF ** -0.5, 0.09375, ((0, 4),)),
        "down_bias": bell_draw(splits[15], (D,), 0.5, 3.0, ((0, 4),)),
    }


@jax.custom_vjp
def low(v):
    return lax.optimization_barrier(v.astype(jnp.bfloat16)).astype(jnp.float32)

@jax.custom_vjp
def low_back(v):
    return v

def low_keep(v):
    return (low(v), None)

def low_pass(kept, grad):
    return (grad,)

def back_keep(v):
    return (v, None)

def back_low(kept, grad):
    return (low(grad),)
low.defvjp(low_keep, low_pass)
low_back.defvjp(back_keep, back_low)
EPS = 1e-05
FULL_PRECISION = lax.Precision.HIGHEST

def layer_norm(values, gain, shift):
    average = lax.optimization_barrier(jnp.mean(values, axis=-1, keepdims=True))
    centered = values - average
    variance = lax.optimization_barrier(jnp.mean(centered * centered, axis=-1, keepdims=True))
    return centered * lax.rsqrt(variance + EPS) * gain + shift

def angles_of(positions):
    pairs = ROT // 2
    freqs = jnp.exp(jnp.arange(pairs, dtype=jnp.float32) * (-2.0 * math.log(10000.0) / ROT))
    angle = positions.astype(jnp.float32)[..., None] * freqs
    return (jnp.cos(angle)[..., None, :], jnp.sin(angle)[..., None, :])

def rotate(values, cosine, sine):
    pairs = ROT // 2
    first = values[..., :pairs]
    second = values[..., pairs:ROT]
    return jnp.concatenate([first * cosine - second * sine, second * cosine + first * sine, values[..., ROT:]], axis=-1)

def attend(packed):
    query, key, value, positions = packed
    scores = low_back(jnp.einsum('qhc,khc->hqk', query, key, precision=FULL_PRECISION) * HEAD ** (-0.5))
    allowed = positions[:, None] >= positions[None, :]
    scores = jnp.where(allowed[None], scores, -1e+30)
    row_max = lax.optimization_barrier(jnp.max(scores, axis=-1, keepdims=True))
    powers = jnp.exp(scores - row_max)
    probs = low(powers / lax.optimization_barrier(jnp.sum(powers, axis=-1, keepdims=True)))
    return jnp.einsum('hqk,khc->qhc', probs, value, precision=FULL_PRECISION)

def forward(params, inputs, positions):
    gain_one, shift_one, gain_two, shift_two, query_key_value_weight, query_bias, value_bias, output_projection_weight, output_projection_bias, up_projection_weight, up_projection_bias, down_projection_weight, down_projection_bias = params
    seq_here, length = positions.shape
    first_hidden_state = low(layer_norm(inputs, gain_one, shift_one))
    second_hidden_state = low(layer_norm(inputs, gain_two, shift_two))
    projected_output = jnp.einsum('aoq,qy->aoy', first_hidden_state, query_key_value_weight, precision=FULL_PRECISION)
    query_pre = low_back(projected_output[..., :D] + query_bias).reshape(seq_here, length, HEADS, HEAD)
    key_pre = low_back(projected_output[..., D:2 * D]).reshape(seq_here, length, HEADS, HEAD)
    value = low_back(low(projected_output[..., 2 * D:] + value_bias)).reshape(seq_here, length, HEADS, HEAD)
    cosine, sine = angles_of(positions)
    query = low(rotate(query_pre, cosine, sine))
    key = low(rotate(key_pre, cosine, sine))
    attended = lax.map(jax.checkpoint(attend), (query, key, value, positions))
    attention_mixture = low_back(low(attended.reshape(seq_here, length, D)))
    attention_output = jnp.einsum('aoq,qy->aoy', attention_mixture, output_projection_weight, precision=FULL_PRECISION) + output_projection_bias
    before_activation = low_back(jnp.einsum('aoq,qy->aoy', second_hidden_state, up_projection_weight, precision=FULL_PRECISION) + up_projection_bias)
    activation_values = low(jax.nn.gelu(before_activation, approximate=False))
    perceptron_output = jnp.einsum('jtu,uz->jtz', activation_values, down_projection_weight, precision=FULL_PRECISION) + down_projection_bias
    return inputs + attention_output + perceptron_output

def reference(tokens, cotangent, block_of, ln1_gain, ln1_bias, ln2_gain, ln2_bias, w_qkv, q_bias, v_bias, w_out, out_bias, w_up, up_bias, w_down, down_bias):
    params = tuple((p.astype(jnp.float32) for p in (ln1_gain, ln1_bias, ln2_gain, ln2_bias, w_qkv, q_bias, v_bias, w_out, out_bias, w_up, up_bias, w_down, down_bias)))

    def to_seqs(values):
        shaped = values.astype(jnp.float32).reshape(N_REP, N_SHARD, SEQS, 2 * BLOCK_LEN, D)
        return shaped.transpose(0, 2, 1, 3, 4).reshape(N_REP, SEQS, BLOCKS * BLOCK_LEN, D)

    def from_seqs(values):
        shaped = values.reshape(N_REP, SEQS, N_SHARD, 2 * BLOCK_LEN, D)
        return shaped.transpose(0, 2, 1, 3, 4).reshape(TOKENS, D)
    inputs = to_seqs(tokens)
    grads_in = to_seqs(cotangent)
    offsets = jnp.arange(BLOCK_LEN, dtype=jnp.int32)
    positions = (block_of.astype(jnp.int32).reshape(N_REP, SEQS, BLOCKS)[..., None] * BLOCK_LEN + offsets).astype(jnp.int32)
    positions = positions.reshape(N_REP, SEQS, BLOCKS * BLOCK_LEN)

    def step(totals, packed):
        group_in, group_grad, group_pos = packed
        result, pull = jax.vjp(lambda prm, val: forward(prm, val, group_pos), params, group_in)
        param_grads, input_grads = pull(group_grad)
        totals = tuple((a + b for a, b in zip(totals, param_grads)))
        return (totals, (result, input_grads))
    zeros = tuple((jnp.zeros_like(p) for p in params))
    totals, (results, input_grads) = lax.scan(step, zeros, (inputs, grads_in, positions))
    output = from_seqs(results).astype(jnp.bfloat16)
    input_grad = from_seqs(input_grads)
    return (output, input_grad, totals[0], totals[1], totals[2], totals[3], totals[4], totals[5], totals[6], totals[7], totals[8], totals[9], totals[10], totals[11], totals[12])
```

```python
import functools, math
import jax, jax.numpy as jnp
from jax import lax
from jax.experimental import pallas as pl
from jax.experimental.pallas import tpu as pltpu
HEADS=16;HEAD=64;ROT=16
NEG=-1e30
bf=jnp.bfloat16; f32=jnp.float32
def dot(a,b,ca,cb):
    return lax.dot_general(a,b,(((ca,),(cb,)),((),())),preferred_element_type=f32)

def attn_kernel(loc_ref, qkv_ref, dm_ref, qb_ref, vb_ref, tab_ref,
                mixed_ref, dqkv_ref, dbias_ref, qs, ks, vs, gs, dq_acc, dk_acc, dv_acc, *, nb, blk, heads, qblk):
    seq = pl.program_id(0)
    W = heads*HEAD
    L = nb*blk
    def rope(x, b, d):
        c = tab_ref[0, b*blk:(b+1)*blk, :]; sa = tab_ref[1, b*blk:(b+1)*blk, :]; sb = tab_ref[2, b*blk:(b+1)*blk, :]
        return x*c + d*(pltpu.roll(x, W-ROT//2, 1)*sa + pltpu.roll(x, ROT//2, 1)*sb)
    for b in range(nb):
        r = loc_ref[seq, b]
        rows = pl.ds(b*blk, blk)
        blkv = qkv_ref[r]
        qs[rows,:] = rope(blkv[:, :W] + qb_ref[...], b, 1.0).astype(bf)
        ks[rows,:] = rope(blkv[:, W:2*W], b, 1.0).astype(bf)
        vs[rows,:] = (blkv[:, 2*W:] + vb_ref[...]).astype(bf)
        gs[rows,:] = dm_ref[r]
    dk_acc[...] = jnp.zeros_like(dk_acc)
    dv_acc[...] = jnp.zeros_like(dv_acc)
    scale = HEAD**-0.5
    lane = lax.broadcasted_iota(jnp.int32,(1,W),1)//HEAD
    for qi in range(L//qblk):
        q0=qi*qblk; kmax=q0+qblk
        qrows=pl.ds(q0,qblk)
        tri = (lax.broadcasted_iota(jnp.int32,(qblk,qblk),0) >= lax.broadcasted_iota(jnp.int32,(qblk,qblk),1))
        def head(h, carry):
            o_sum, dq_sum = carry
            m = (lane==h)
            q = jnp.where(m, qs[qrows,:], jnp.zeros((),bf))
            g = jnp.where(m, gs[qrows,:], jnp.zeros((),bf))
            k = ks[pl.ds(0,kmax),:]; v = vs[pl.ds(0,kmax),:]
            s = dot(q,k,1,1)*scale
            sd = jnp.where(tri, s[:,q0:], NEG)
            s = jnp.concatenate([s[:,:q0],sd],axis=1) if q0 else sd
            mx = jnp.max(s,axis=1,keepdims=True)
            p = jnp.exp(s-mx)
            p = p*(1.0/jnp.sum(p,axis=1,keepdims=True))
            pb = p.astype(bf)
            o = dot(pb, v,1,0)
            dv_acc[pl.ds(0,kmax),:] += dot(pb,g,0,0)
            dp = dot(g,v,1,1)
            ds = (p*(dp-jnp.sum(dp*p,axis=1,keepdims=True))).astype(bf)
            dq = dot(ds,k,1,0)
            dk_acc[pl.ds(0,kmax),:] += dot(ds,q,0,0)
            mf = m.astype(f32)
            return (o_sum+o*mf, dq_sum+dq*mf)
        z=jnp.zeros((qblk,W),f32)
        o,dq = lax.fori_loop(0,heads,head,(z,z))
        dq_acc[qrows,:]=dq
        for t in range(qblk//blk):
            r = loc_ref[seq, qi*(qblk//blk)+t]
            mixed_ref[r] = o[t*blk:(t+1)*blk,:].astype(bf)
    dqs=jnp.zeros((1,W),f32); dvs=jnp.zeros((1,W),f32)
    for b in range(nb):
        r = loc_ref[seq, b]; rows=pl.ds(b*blk,blk)
        dqb = rope(dq_acc[rows,:]*scale, b, -1.0).astype(bf)
        dkb = rope(dk_acc[rows,:]*scale, b, -1.0).astype(bf)
        dvb = dv_acc[rows,:].astype(bf)
        dqkv_ref[r] = jnp.concatenate([dqb,dkb,dvb],axis=1)
        dqs += jnp.sum(dqb.astype(f32),axis=0,keepdims=True)
        dvs += jnp.sum(dvb.astype(f32),axis=0,keepdims=True)
    add = jnp.concatenate([dqs,dvs],axis=1)
    @pl.when(seq==0)
    def _(): dbias_ref[...] = add
    @pl.when(seq!=0)
    def _(): dbias_ref[...] += add

def attention(loc, qkv, dm, qb, vb, tab, qblk=256):
    n, blk, w3 = qkv.shape
    W=w3//3; heads=W//HEAD
    seqs, nb = loc.shape
    L=nb*blk
    whole=lambda shape: pl.BlockSpec(shape, lambda s,*_: (0,)*len(shape))
    return pl.pallas_call(
        functools.partial(attn_kernel, nb=nb, blk=blk, heads=heads, qblk=qblk),
        grid_spec=pltpu.PrefetchScalarGridSpec(num_scalar_prefetch=1, grid=(seqs,),
            in_specs=[whole((n,blk,w3)), whole((n,blk,W)), whole((1,W)), whole((1,W)), whole((3,L,W))],
            out_specs=[whole((n,blk,W)), whole((n,blk,w3)), whole((1,2*W))],
            scratch_shapes=[pltpu.VMEM((L,W),bf)]*4+[pltpu.VMEM((L,W),f32)]*3),
        out_shape=[jax.ShapeDtypeStruct((n,blk,W),bf), jax.ShapeDtypeStruct((n,blk,w3),bf), jax.ShapeDtypeStruct((1,2*W),f32)],
        compiler_params=pltpu.CompilerParams(dimension_semantics=("arbitrary",), vmem_limit_bytes=60*2**20),
        cost_estimate=pl.CostEstimate(flops=2*6*seqs*heads*L*L*64, bytes_accessed=n*blk*w3*6, transcendentals=seqs*heads*L*L//2),
        name="attention",
    )(loc, qkv, dm, qb, vb, tab)

def tables(L, W):
    pairs=ROT//2
    lane=jnp.arange(W)%HEAD
    freqs=jnp.exp((lane%pairs).astype(f32)*(-2.0*math.log(10000.0)/ROT))
    ang=jnp.arange(L,dtype=jnp.int32).astype(f32)[:,None]*freqs[None]
    c=jnp.where(lane<ROT, jnp.cos(ang), 1.0); s=jnp.sin(ang)
    sa=jnp.where(lane<pairs,-s,0.0); sb=jnp.where((lane>=pairs)&(lane<ROT),s,0.0)
    return jnp.stack([c,sa,sb])


from jax.sharding import PartitionSpec as P

EPS = 1e-05


def normalize(values):
    average = jnp.mean(values, axis=-1, keepdims=True)
    centered = values - average
    inverse = lax.rsqrt(jnp.mean(centered * centered, axis=-1, keepdims=True) + EPS)
    return (centered * inverse, inverse)


def outer(left, right):
    return dot(left, right, 0, 0)


def times_t(left, right):
    return dot(left, right, 1, 1)


def times(left, right):
    return dot(left, right, 1, 0)


def per_device(rep_size, shard_size, tokens, cotangent, block_of, ln1_gain, ln1_bias, ln2_gain,
               ln2_bias, w_qkv, q_bias, v_bias, w_out, out_bias, w_up, up_bias, w_down, down_bias):
    rows, width = tokens.shape
    part = ln1_gain.shape[0]
    hidden = up_bias.shape[0]
    seqs, slots = block_of.shape
    blk = rows // seqs // 2
    me = lax.axis_index("shard")
    rep = lax.axis_index("rep")

    def swap(x, k, axis="shard"):
        size = shard_size if axis == "shard" else rep_size
        return lax.ppermute(x, axis, [(i, i ^ k) for i in range(size)])

    def gather_pieces(x):
        across = swap(x, 2)
        return [x, swap(x, 1), across, swap(across, 1)]

    small = jnp.stack([ln1_gain, ln1_bias, ln2_gain, ln2_bias, out_bias, down_bias])
    small = jnp.concatenate([small.reshape(-1), jnp.zeros((2 * width - 6 * part,), bf)]) if False else small
    qkv_blocks = w_qkv.reshape(part, 3, shard_size, part)

    def block_for(d):
        up = lax.dynamic_slice_in_dim(w_up, d * hidden, hidden, 1)
        qkv = lax.dynamic_index_in_dim(qkv_blocks, d, 2, keepdims=False).reshape(part, 3 * part)
        return jnp.concatenate([qkv, up], axis=1)

    token_pieces = gather_pieces(tokens)
    small_pieces = gather_pieces(small)
    weight_pieces = [block_for(me)] + [swap(block_for(me ^ k), k) for k in (1, 2, 3)]
    cot_pieces = gather_pieces(cotangent)

    def ordered(pieces):
        stacked = jnp.stack(pieces)
        return [lax.dynamic_index_in_dim(stacked, me ^ j, 0, keepdims=False) for j in range(shard_size)]

    vectors = jnp.stack(ordered(small_pieces), axis=1).reshape(6, width).astype(f32)
    gain_one, shift_one, gain_two, shift_two, obias, dbias = [vectors[i][None] for i in range(6)]
    weights = jnp.concatenate(ordered(weight_pieces), axis=0)
    wqkv = weights[:, : 3 * part]
    wup = weights[:, 3 * part :]

    x = jnp.concatenate(token_pieces, axis=0).astype(f32)
    dy = jnp.concatenate(cot_pieces, axis=0)
    total = x.shape[0]
    blocks = total // blk

    slot_at = jnp.argsort(block_of, axis=1).astype(jnp.int32)
    place = ((slot_at // 2) ^ me) * (2 * seqs) + jnp.arange(seqs, dtype=jnp.int32)[:, None] * 2 + slot_at % 2

    normed, inverse = normalize(x)
    h_one = (normed * gain_one + shift_one).astype(bf)
    h_two = (normed * gain_two + shift_two).astype(bf)
    projected = times(h_one, wqkv)
    pre = times(h_two, wup) + up_bias.astype(f32)
    act, gelu_pull = jax.vjp(lambda p: jax.nn.gelu(p, approximate=False), pre)
    act = act.astype(bf)
    d_mixed = times_t(dy, w_out).astype(bf)
    d_act = times_t(dy, w_down)
    d_pre = gelu_pull(d_act)[0].astype(bf)
    g_down = outer(act, dy)
    g_up = outer(h_two, d_pre)
    d_h_two = times_t(d_pre, wup)
    mixed, d_qkv, d_bias = attention(
        place, projected.reshape(blocks, blk, 3 * part), d_mixed.reshape(blocks, blk, part),
        q_bias.astype(f32)[None], v_bias.astype(f32)[None], tables(slots * blk, part))
    mixed = mixed.reshape(total, part)
    d_qkv = d_qkv.reshape(total, 3 * part)
    partial_out = (times(mixed, w_out) + times(act, w_down)).astype(bf)
    g_out = outer(mixed, dy)
    g_qkv = outer(h_one, d_qkv)
    d_h_one = times_t(d_qkv, wqkv)

    ln_grads = jnp.stack([
        jnp.sum(d_h_one * normed, axis=0), jnp.sum(d_h_one, axis=0),
        jnp.sum(d_h_two * normed, axis=0), jnp.sum(d_h_two, axis=0)])
    partial_f = (d_h_one * gain_one + d_h_two * gain_two).astype(bf)

    def scatter_rows(pieces):
        got = swap(jnp.concatenate([pieces[1], pieces[3]], axis=0), 1)
        n = pieces[0].shape[0]
        mine = pieces[0].astype(f32) + got[:n].astype(f32)
        theirs = (pieces[2].astype(f32) + got[n:].astype(f32)).astype(bf)
        return mine + swap(theirs, 2).astype(f32)

    def split(a):
        return [a[k * rows : (k + 1) * rows] for k in range(shard_size)]

    out_sum = scatter_rows(split(partial_out))
    own_x = tokens.astype(f32)
    output = (own_x + out_sum + obias + dbias).astype(bf)

    ln_cut = ln_grads.astype(bf).reshape(4, shard_size, part).transpose(1, 0, 2).reshape(shard_size, 4 * part)
    ln_rows = [jnp.broadcast_to(lax.dynamic_index_in_dim(ln_cut, me ^ k, 0), (16, width)) for k in range(shard_size)]
    f_sum = scatter_rows([jnp.concatenate([p, r], axis=0) for p, r in zip(split(partial_f), ln_rows)])
    ln_mine = f_sum[rows]
    f_sum = f_sum[:rows]
    own_normed, own_inverse = normalize(own_x)
    own_dy = cotangent.astype(f32)
    input_grad = own_dy + own_inverse * (
        f_sum - jnp.mean(f_sum, axis=-1, keepdims=True)
        - own_normed * jnp.mean(f_sum * own_normed, axis=-1, keepdims=True))

    bits = []
    b = 1
    while b < rep_size:
        bits.append(b)
        b *= 2

    def halves(a, bit):
        n = a.shape[0] // 2
        own = (rep // bit) % 2
        keep = lax.dynamic_slice_in_dim(a, own * n, n, 0)
        give = lax.dynamic_slice_in_dim(a, (1 - own) * n, n, 0)
        return keep, give

    def reduce_rep(a):
        for bit in bits:
            keep, give = halves(a, bit)
            a = keep.astype(f32) + swap(give.astype(bf), bit, "rep").astype(f32)
        return a

    def gather_rep(a):
        for bit in reversed(bits):
            own = (rep // bit) % 2
            got = swap(a, bit, "rep")
            pair = jnp.stack([a, got])
            lo = lax.dynamic_index_in_dim(pair, own, 0, keepdims=False)
            hi = lax.dynamic_index_in_dim(pair, 1 - own, 0, keepdims=False)
            a = jnp.concatenate([lo, hi], axis=0)
        return a

    def to_rows(a):
        pieces = [lax.dynamic_index_in_dim(a, me, 0, keepdims=False)]
        pieces += [swap(lax.dynamic_index_in_dim(a, me ^ k, 0, keepdims=False), k) for k in (1, 2, 3)]
        return jnp.stack(ordered(pieces), axis=1)

    r8 = rep_size
    cut = part // r8
    batch = jnp.concatenate([
        g_down.reshape(r8, shard_size * cut, width),
        g_up.reshape(shard_size, r8, cut, hidden).transpose(1, 0, 2, 3).reshape(r8, shard_size * cut, hidden)], axis=1).astype(bf)
    red = reduce_rep(batch)[0].astype(bf)
    n = shard_size * cut
    up_rows = to_rows(red[n:].reshape(shard_size, cut, hidden))
    back = jnp.concatenate([red[:n], up_rows.reshape(n, hidden)], axis=0)[None]
    full = gather_rep(back)
    grad_down = full[:, :n].reshape(hidden, width).astype(f32)
    grad_up = full[:, n:].reshape(part, shard_size * hidden).astype(f32)

    w3 = 3 * part
    g_qkv8 = g_qkv.reshape(shard_size, r8, cut, w3).transpose(1, 0, 2, 3).reshape(r8, -1, width)
    batch2 = jnp.concatenate([g_out.reshape(r8, cut, width), g_qkv8], axis=1).astype(bf)
    red2 = reduce_rep(batch2)[0].astype(bf)
    qkv_rows = to_rows(red2[cut:].reshape(shard_size, cut, w3))
    qkv_rows = qkv_rows.reshape(cut, shard_size, 3, part).transpose(0, 2, 1, 3).reshape(-1, width)
    full2 = gather_rep(jnp.concatenate([red2[:cut], qkv_rows], axis=0)[None])
    grad_out = full2[:, :cut].reshape(part, width).astype(f32)
    grad_qkv = full2[:, cut:].reshape(part, 3 * width).astype(f32)

    dy_sum = lax.dynamic_slice_in_dim(jnp.sum(dy.astype(f32), axis=0), me * part, part, 0)
    up_sum = jnp.sum(d_pre.astype(f32), axis=0)
    vec = jnp.concatenate([ln_mine, up_sum, d_bias[0], dy_sum])
    vec = lax.psum(vec, "rep")
    o = width
    return (
        output, input_grad, vec[:part], vec[part : 2 * part], vec[2 * part : 3 * part], vec[3 * part : 4 * part],
        grad_qkv, vec[o + hidden : o + hidden + part], vec[o + hidden + part : o + hidden + 2 * part],
        grad_out, vec[o + hidden + 2 * part :], grad_up, vec[o : o + hidden], grad_down, vec[o + hidden + 2 * part :])


def solution(mesh):
    row = P(("rep", "shard"), None)
    one, two = P("shard"), P("shard", None)
    return jax.shard_map(
        functools.partial(per_device, mesh.shape["rep"], mesh.shape["shard"]),
        mesh=mesh,
        in_specs=(row, row, P("rep", None), one, one, one, one, two, one, one, two, one, two, one, two, one),
        out_specs=(row, row, one, one, one, one, two, one, one, two, one, two, one, two, one),
        check_vma=False,
    )
```
